768 devices in a mesh: segment: 2 (over core), lon: 48 (over y_hi, z), lat: 8 (over y_lo, x).
Axes of the slice: x: 4, y: 8 (y_hi: 4, y_lo: 2; y = y_hi * 2 + y_lo), z: 12, core: 2. Of those that a mesh axis runs over, the one named last changes fastest.
Arguments:
- dec_cot: bfloat16 [2, 768, 192, 128], P('segment', 'lon', 'lat'), may hold values from -6 to 6
- saved_conv: bfloat16 [2, 4, 768, 192, 256], P('segment', None, 'lon', 'lat'), may hold values from -6 to 6
- dec_weight: bfloat16 [256, 128], replicated, may hold values from -0.5 to 0.5
- w_in: bfloat16 [4, 256, 512], replicated, may hold values from -0.375 to 0.375
- w_out: bfloat16 [4, 512, 256], replicated, may hold values from -0.25 to 0.25
- conv_taps: float32 [4, 5, 256], replicated, may hold values from -3 to 3
- dilation: int32 [4], replicated, may hold values from 1 to 48, as said below
Outputs:
- in_adjoint: bfloat16 [2, 768, 192, 256], P('segment', 'lon', 'lat')
The draws below stay inside these ranges and needn't reach their ends.
Inputs may be any that keep to these rules, and one draw needn't show every extreme that they name: Every layer's dilation lies in 1 to 48; at least one layer has exactly 48.
All inputs are finite; a program needn't handle non-finite values.
Results may differ from the reference program's by a relative error of at most 0.013.
Values may be sent and summed in bfloat16 or wider, within the bound.
A program may use at most 32 MiB of HBM per device.

```python
import jax
import jax.numpy as jnp
from jax import lax

C = 256
H = 512
V = 128
LAYERS = 4
CL = 16
NLON = 768
NLAT = 192
N_SEGMENT = 2


def draw_dilation(key, part):
    first_key, second_key = jax.random.split(jax.random.fold_in(key, 11))
    values = jax.random.randint(first_key, (LAYERS,), 1, 3 * CL + 1)
    chosen = jax.random.randint(second_key, (), 0, LAYERS)
    return jnp.where(jnp.arange(LAYERS) == chosen, 3 * CL, values).astype(jnp.int32)


def shard_levels(own_key, extent, shards, low, top_value):
    def one(position, parts):
        steps = jax.random.uniform(jax.random.fold_in(jax.random.fold_in(own_key, 6), position), (parts,), jnp.float32, low / len(shards), top_value / len(shards))
        return jnp.repeat(jnp.exp(steps), extent[position] // parts).reshape((-1,) + (1,) * (len(extent) - position - 1))

    gain = one(*shards[0])
    for cut in shards[1:]:
        gain = gain * one(*cut)
    return gain


def noise(stream_key, shape, width, bound, cuts=(), kind=jnp.bfloat16):
    gain = shard_levels(stream_key, shape, cuts, -0.22, 0.18) if cuts else 1.0
    result = jax.random.normal(stream_key, shape, jnp.float32) * width * gain
    return jnp.minimum(jnp.maximum(result, -bound), bound).astype(kind)


def setup_inputs(seed: int = 0) -> dict:
    seeds = jax.random.split(jax.random.key(seed), 8)
    dec_cot = noise(seeds[0], (N_SEGMENT, NLON, NLAT, V), 1.0, 6.0, ((0, 2), (1, 48), (2, 8)))
    saved_conv = noise(seeds[1], (N_SEGMENT, LAYERS, NLON, NLAT, C), 1.0, 6.0, ((0, 2), (2, 48), (3, 8)))
    dec_weight = noise(seeds[2], (C, V), V ** -0.5, 0.5)
    w_in = noise(seeds[3], (LAYERS, C, H), C ** -0.5, 0.375)
    w_out = noise(seeds[4], (LAYERS, H, C), H ** -0.5, 0.25)
    conv_taps = noise(seeds[5], (LAYERS, 5, C), 0.5, 3.0, (), jnp.float32)
    dilation = draw_dilation(jax.random.fold_in(seeds[7], 71), 0)
    return {"dec_cot": dec_cot, "saved_conv": saved_conv, "dec_weight": dec_weight, "w_in": w_in, "w_out": w_out, "conv_taps": conv_taps, "dilation": dilation}


def gelu_slope(hidden):
    normal_cdf = 0.5 * (1.0 + jax.scipy.special.erf(hidden * 0.7071067811865476))
    density = jnp.exp(-0.5 * hidden * hidden) * 0.3989422804014327
    return normal_cdf + hidden * density


def reference(dec_cot, saved_conv, dec_weight, w_in, w_out, conv_taps, dilation):
    results = []
    for slot_index in range(2):
        handed_cot = dec_cot[1 - slot_index].reshape(-1, V)
        handed = jnp.dot(handed_cot, dec_weight.T, preferred_element_type=jnp.float32).astype(jnp.bfloat16)
        gradient = lax.optimization_barrier(handed).astype(jnp.float32)
        for layer_index in reversed(range(LAYERS)):
            conv_out = saved_conv[slot_index, layer_index].reshape(-1, C)
            hidden = jnp.dot(conv_out, w_in[layer_index], preferred_element_type=jnp.float32)
            cot_low = gradient.astype(jnp.bfloat16)
            act_grad = jnp.dot(cot_low, w_out[layer_index].T, preferred_element_type=jnp.float32)
            pre_grad = (act_grad * gelu_slope(hidden)).astype(jnp.bfloat16)
            conv_grad = jnp.dot(pre_grad, w_in[layer_index].T, preferred_element_type=jnp.float32).astype(jnp.bfloat16)
            field = conv_grad.reshape(NLON, NLAT, C).astype(jnp.float32)
            taps_now = conv_taps[layer_index]
            offset = dilation[layer_index]
            lat_padded = jnp.pad(field, ((0, 0), (1, 1), (0, 0)))
            zonal = taps_now[0] * jnp.roll(field, -offset, axis=0) + taps_now[2] * jnp.roll(field, offset, axis=0)
            zonal = lax.optimization_barrier(zonal.astype(jnp.bfloat16)).astype(jnp.float32)
            tapped = zonal + taps_now[1] * field + taps_now[3] * lat_padded[:, 2:] + taps_now[4] * lat_padded[:, :-2]
            gradient = gradient + tapped.reshape(-1, C)
        results.append(gradient.reshape(NLON, NLAT, C).astype(jnp.bfloat16))
    return jnp.stack(results)
```

```python
import functools

import jax
import jax.numpy as jnp
from jax import lax
from jax.experimental import pallas as pl
from jax.experimental.pallas import tpu as pltpu
from jax.sharding import PartitionSpec as P

MESH = pl.DeviceIdType.MESH
ROWS = 8
PIECES = 2


def gelu_slope(hidden):
    normal_cdf = 0.5 * (1.0 + lax.erf(hidden * 0.7071067811865476))
    density = jnp.exp(-0.5 * hidden * hidden) * 0.3989422804014327
    return normal_cdf + hidden * density


def against(left, right):
    return lax.dot_general(
        left, right, (((1,), (1,)), ((), ())), preferred_element_type=jnp.float32
    )


def hop_cells(reach, cells):
    counts = []
    while reach > 0:
        counts.append(min(reach, cells))
        reach -= cells
    return counts


def kernel(
    dims,
    reaches,
    dilation_ref,
    dec_cot_ref,
    saved_ref,
    dec_weight_ref,
    w_in_ref,
    w_out_ref,
    taps_ref,
    out_ref,
    *scratch,
):
    layers, cells, lats, chans, hidden_units, lon_count, lat_count = dims
    chunks = lats // ROWS
    zonal = [scratch[l * chunks : (l + 1) * chunks] for l in range(layers)]
    (
        ahead_halo,
        behind_halo,
        dec_here,
        dec_weight,
        saved,
        w_in,
        w_out,
        slope,
        grad,
        load_sem,
        dec_sem,
        hop_send,
        hop_recv,
        lat_send,
        lat_recv,
    ) = scratch[layers * chunks :]

    seg = lax.axis_index("segment")
    lon = lax.axis_index("lon")
    lat = lax.axis_index("lat")
    east = lax.rem(lon + 1, lon_count)
    west = lax.rem(lon + lon_count - 1, lon_count)
    north = lax.rem(lat + 1, lat_count)
    south = lax.rem(lat + lat_count - 1, lat_count)

    barrier = pltpu.get_barrier_semaphore()
    for peer in (
        {"segment": 1 - seg},
        {"lon": east},
        {"lon": west},
        {"lat": north},
        {"lat": south},
    ):
        pl.semaphore_signal(barrier, inc=1, device_id=peer, device_id_type=MESH)

    loads = {}

    def load(name, src, dst):
        loads[name] = pltpu.make_async_copy(src, dst, load_sem.at[len(loads)])
        loads[name].start()

    for l in reversed(range(layers)):
        load(("saved", l), saved_ref.at[l], saved.at[l])
        load(("w_in", l), w_in_ref.at[l], w_in.at[l])
        if l == layers - 1:
            load("dec_weight", dec_weight_ref, dec_weight)
        load(("w_out", l), w_out_ref.at[l], w_out.at[l])

    def slope_piece(l, piece):
        if piece == 0:
            loads["saved", l].wait()
            loads["w_in", l].wait()
        span = cells // PIECES
        rows = span * lats
        hidden = jnp.dot(
            saved[l, pl.ds(piece * rows, rows), :],
            w_in[l],
            preferred_element_type=jnp.float32,
        )
        slope[l, pl.ds(piece * span, span)] = gelu_slope(hidden).reshape(
            span, lats, hidden_units
        )

    pl.semaphore_wait(barrier, 5)
    dec_copy = pltpu.make_async_remote_copy(
        src_ref=dec_cot_ref,
        dst_ref=dec_here,
        send_sem=dec_sem.at[0],
        recv_sem=dec_sem.at[1],
        device_id={"segment": 1 - seg},
        device_id_type=MESH,
    )
    dec_copy.start()
    for piece in range(PIECES):
        slope_piece(layers - 1, piece)
    loads["dec_weight"].wait()
    dec_copy.wait()
    handed = against(dec_here[...], dec_weight[...]).astype(jnp.bfloat16)
    grad[...] = handed.astype(jnp.float32).reshape(cells, lats, chans)

    hop_copies = {}

    def start_hop(l, c, hop):
        counts = hop_cells(reaches[l], cells)
        if hop >= len(counts):
            return
        count, reach, buf = counts[hop], reaches[l], zonal[l][c]
        hops = len(counts)
        slot = (l * chunks + c) * 6 + hop * 2
        own = reach + hop * cells
        to_west = pltpu.make_async_remote_copy(
            src_ref=buf.at[pl.ds(own, count)],
            dst_ref=buf.at[pl.ds(own + cells, count)],
            send_sem=hop_send.at[slot],
            recv_sem=hop_recv.at[slot],
            device_id={"lon": west},
            device_id_type=MESH,
        )
        own = reach - hop * cells + cells - count
        to_east = pltpu.make_async_remote_copy(
            src_ref=buf.at[pl.ds(own, count)],
            dst_ref=buf.at[pl.ds(own - cells, count)],
            send_sem=hop_send.at[slot + 1],
            recv_sem=hop_recv.at[slot + 1],
            device_id={"lon": east},
            device_id_type=MESH,
        )
        to_west.start()
        to_east.start()
        hop_copies[l, c, hop] = (to_west, to_east)

    def arrive(l, c, hop):
        for copy in hop_copies.get((l, c, hop), ()):
            copy.wait_recv()

    lat_copies = {}

    def start_lat(l, c):
        own = zonal[l][c].at[pl.ds(reaches[l], cells)]
        for which, chunk, peer, halo in (
            (0, 0, south, ahead_halo),
            (1, chunks - 1, north, behind_halo),
        ):
            if c == chunk:
                copy = pltpu.make_async_remote_copy(
                    src_ref=own,
                    dst_ref=halo.at[l],
                    send_sem=lat_send.at[2 * l + which],
                    recv_sem=lat_recv.at[2 * l + which],
                    device_id={"lat": peer},
                    device_id_type=MESH,
                )
                copy.start()
                lat_copies[l, which] = copy

    def conv_grad(l, c):
        if c == 0:
            loads["w_out", l].wait()
        rows = pl.ds(c * ROWS, ROWS)
        low = grad[:, rows, :].reshape(cells * ROWS, chans).astype(jnp.bfloat16)
        act = against(low, w_out[l])
        steep = slope[l, :, rows, :].reshape(cells * ROWS, hidden_units)
        pre = (act * steep).astype(jnp.bfloat16)
        result = against(pre, w_in[l]).reshape(cells, ROWS, chans)
        zonal[l][c][pl.ds(reaches[l], cells)] = result.astype(jnp.bfloat16)
        start_hop(l, c, 0)
        start_lat(l, c)

    def field(l, c):
        return zonal[l][c][pl.ds(reaches[l], cells)].astype(jnp.float32)

    def tapped(l, c):
        taps = [taps_ref[t, l, :].reshape(1, 1, chans) for t in range(5)]
        offset = dilation_ref[l]
        reach = reaches[l]
        place = lax.broadcasted_iota(jnp.int32, (cells, ROWS, chans), 1)
        here = field(l, c)
        if c + 1 < chunks:
            after = field(l, c + 1)
        else:
            after = ahead_halo[l].astype(jnp.float32)
            after = jnp.where(lat == lat_count - 1, jnp.zeros_like(after), after)
        if c > 0:
            before = field(l, c - 1)
        else:
            before = behind_halo[l].astype(jnp.float32)
            before = jnp.where(lat == 0, jnp.zeros_like(before), before)
        next_row = pltpu.roll(jnp.where(place == 0, after, here), ROWS - 1, 1)
        last_row = pltpu.roll(jnp.where(place == ROWS - 1, before, here), 1, 1)
        window = zonal[l][c]
        ahead = window[pl.ds(reach + offset, cells)].astype(jnp.float32)
        behind = window[pl.ds(reach - offset, cells)].astype(jnp.float32)
        both = (taps[0] * ahead + taps[2] * behind).astype(jnp.bfloat16)
        return (
            both.astype(jnp.float32)
            + taps[1] * here
            + (taps[3] * next_row + taps[4] * last_row)
        )

    for c in range(chunks):
        conv_grad(layers - 1, c)

    for l in reversed(range(layers)):
        hops = len(hop_cells(reaches[l], cells))
        for c in range(chunks):
            arrive(l, c, 0)
            start_hop(l, c, 1)
            if l > 0 and c < PIECES:
                slope_piece(l - 1, c)
        for hop in range(1, hops - 1):
            for c in range(chunks):
                arrive(l, c, hop)
                start_hop(l, c, hop + 1)
        for which in (1, 0):
            lat_copies[l, which].wait_recv()
        for c in range(chunks):
            if hops > 1:
                arrive(l, c, hops - 1)
            rows = pl.ds(c * ROWS, ROWS)
            total = grad[:, rows, :] + tapped(l, c)
            if l > 0:
                grad[:, rows, :] = total
                conv_grad(l - 1, c)
            else:
                out_ref[:, rows, :] = total.astype(jnp.bfloat16)

    for copies in hop_copies.values():
        for copy in copies:
            copy.wait_send()
    for copy in lat_copies.values():
        copy.wait_send()


def whole_block(dims, reaches, *operands):
    layers, cells, lats, chans, hidden_units, _, _ = dims
    chunks = lats // ROWS
    dec_rows, values = operands[1].shape
    bf16, f32 = jnp.bfloat16, jnp.float32
    anywhere = pl.BlockSpec(memory_space=pl.ANY)
    return pl.pallas_call(
        functools.partial(kernel, dims, reaches),
        out_shape=jax.ShapeDtypeStruct((cells, lats, chans), bf16),
        in_specs=[
            pl.BlockSpec(memory_space=pltpu.SMEM),
            anywhere,
            anywhere,
            anywhere,
            anywhere,
            anywhere,
            pl.BlockSpec(memory_space=pltpu.VMEM),
        ],
        out_specs=pl.BlockSpec(memory_space=pltpu.VMEM),
        scratch_shapes=[
            pltpu.VMEM((cells + 2 * reaches[l], ROWS, chans), bf16)
            for l in range(layers)
            for c in range(chunks)
        ]
        + [
            pltpu.VMEM((layers, cells, ROWS, chans), bf16),
            pltpu.VMEM((layers, cells, ROWS, chans), bf16),
            pltpu.VMEM((dec_rows, values), bf16),
            pltpu.VMEM((chans, values), bf16),
            pltpu.VMEM((layers, cells * lats, chans), bf16),
            pltpu.VMEM((layers, chans, hidden_units), bf16),
            pltpu.VMEM((layers, hidden_units, chans), bf16),
            pltpu.VMEM((layers, cells, lats, hidden_units), f32),
            pltpu.VMEM((cells, lats, chans), f32),
            pltpu.SemaphoreType.DMA((3 * layers + 1,)),
            pltpu.SemaphoreType.DMA((2,)),
            pltpu.SemaphoreType.DMA((6 * layers * chunks,)),
            pltpu.SemaphoreType.DMA((6 * layers * chunks,)),
            pltpu.SemaphoreType.DMA((2 * layers,)),
            pltpu.SemaphoreType.DMA((2 * layers,)),
        ],
        compiler_params=pltpu.CompilerParams(
            collective_id=0, has_side_effects=True, vmem_limit_bytes=60 << 20
        ),
    )(*operands)


def solution(mesh):
    lon_count, lat_count = mesh.shape["lon"], mesh.shape["lat"]

    def per_device(dec_cot, saved_conv, dec_weight, w_in, w_out, conv_taps, dilation):
        _, layers, cells, lats, chans = saved_conv.shape
        hidden_units = w_in.shape[2]
        dims = (layers, cells, lats, chans, hidden_units, lon_count, lat_count)
        reaches = (3 * cells,) * layers
        out = whole_block(
            dims,
            reaches,
            dilation,
            dec_cot[0].reshape(cells * lats, -1),
            saved_conv[0].reshape(layers, cells * lats, chans),
            dec_weight,
            w_in,
            w_out,
            conv_taps.transpose(1, 0, 2),
        )
        return out[None]

    in_specs = (
        P("segment", "lon", "lat", None),
        P("segment", None, "lon", "lat", None),
        P(),
        P(),
        P(),
        P(),
        P(),
    )
    out_specs = P("segment", "lon", "lat", None)
    return jax.shard_map(
        per_device, mesh=mesh, in_specs=in_specs, out_specs=out_specs, check_vma=False
    )
```

```python
import functools

import jax
import jax.numpy as jnp
from jax import lax
from jax.experimental import pallas as pl
from jax.experimental.pallas import tpu as pltpu
from jax.sharding import PartitionSpec as P

MESH = pl.DeviceIdType.MESH
ROWS = 8
RING = 12
LAG = 2
PIECES = 2


def gelu_slope(hidden):
    normal_cdf = 0.5 * (1.0 + lax.erf(hidden * 0.7071067811865476))
    density = jnp.exp(-0.5 * hidden * hidden) * 0.3989422804014327
    return normal_cdf + hidden * density


def against(left, right):
    return lax.dot_general(
        left, right, (((1,), (1,)), ((), ())), preferred_element_type=jnp.float32
    )


def hop_cells(reach, cells):
    counts = []
    while reach > 0:
        counts.append(min(reach, cells))
        reach -= cells
    return counts


def kernel(
    dims,
    reaches,
    dilation_ref,
    dec_cot_ref,
    saved_ref,
    dec_weight_ref,
    w_in_ref,
    w_out_ref,
    taps_ref,
    out_ref,
    *scratch,
):
    layers, cells, lats, chans, hidden_units, lon_count, lat_count = dims
    chunks = lats // ROWS
    zonal = [scratch[l * chunks : (l + 1) * chunks] for l in range(layers)]
    (
        edge,
        halo,
        dec_here,
        dec_weight,
        saved,
        w_in,
        w_out,
        slope,
        grad,
        load_sem,
        dec_sem,
        hop_send,
        hop_recv,
        via_send,
        lat_send,
        lat_recv,
    ) = scratch[layers * chunks :]

    seg = lax.axis_index("segment")
    lon = lax.axis_index("lon")
    lat = lax.axis_index("lat")
    east = lax.rem(lon + 1, lon_count)
    west = lax.rem(lon + lon_count - 1, lon_count)
    north = lax.rem(lat + 1, lat_count)
    south = lax.rem(lat + lat_count - 1, lat_count)

    def along(steps):
        return lax.rem(lon + lon_count + steps, lon_count)

    place_in_row = lax.rem(lon, RING)
    turns = lat // (lat_count // 2)
    turns_east = turns * (place_in_row // (RING - 1))
    turns_west = turns * ((RING - 1 - place_in_row) // (RING - 1))
    next_row, last_row = along(RING), along(-RING)

    barrier = pltpu.get_barrier_semaphore()
    for peer in (
        {"segment": 1 - seg},
        {"lon": east},
        {"lon": west},
        {"lat": north},
        {"lat": south},
        {"lon": next_row},
        {"lon": last_row},
        {"lon": along(RING - 1)},
        {"lon": along(1 - RING)},
    ):
        pl.semaphore_signal(barrier, inc=1, device_id=peer, device_id_type=MESH)

    loads = {}

    def load(name, src, dst):
        loads[name] = pltpu.make_async_copy(src, dst, load_sem.at[len(loads)])
        loads[name].start()

    for l in reversed(range(layers)):
        load(("saved", l), saved_ref.at[l], saved.at[l])
        load(("w_in", l), w_in_ref.at[l], w_in.at[l])
        if l == layers - 1:
            load("dec_weight", dec_weight_ref, dec_weight)
        load(("w_out", l), w_out_ref.at[l], w_out.at[l])

    def slope_piece(l, piece):
        if piece == 0:
            loads["saved", l].wait()
            loads["w_in", l].wait()
        span = cells // PIECES
        rows = span * lats
        hidden = jnp.dot(
            saved[l, pl.ds(piece * rows, rows), :],
            w_in[l],
            preferred_element_type=jnp.float32,
        )
        slope[l, pl.ds(piece * span, span)] = gelu_slope(hidden).reshape(
            span, lats, hidden_units
        )

    pl.semaphore_wait(barrier, 9)
    dec_copy = pltpu.make_async_remote_copy(
        src_ref=dec_cot_ref,
        dst_ref=dec_here,
        send_sem=dec_sem.at[0],
        recv_sem=dec_sem.at[1],
        device_id={"segment": 1 - seg},
        device_id_type=MESH,
    )
    dec_copy.start()
    for piece in range(PIECES):
        slope_piece(layers - 1, piece)
    loads["dec_weight"].wait()
    dec_copy.wait()
    handed = against(dec_here[...], dec_weight[...]).astype(jnp.bfloat16)
    grad[...] = handed.astype(jnp.float32).reshape(cells, lats, chans)

    order = [c for c in range(chunks) if 0 < c < chunks - 1] + [chunks - 1, 0]
    sent = []
    quick = place_in_row // (RING // 2)
    sides = (quick, 1 - quick)

    def hop_count(l):
        return len(hop_cells(reaches[l], cells))

    def slot_of(l, c, hop):
        return (l * chunks + c) * 3 + hop

    def either(choice, one, other):
        return other + choice * (one - other)

    def hop_copy(l, c, hop, side, turn):
        count, buf = hop_cells(reaches[l], cells)[hop], zonal[l][c]
        slot = slot_of(l, c, hop)
        own = reaches[l] + either(side, cells - count - hop * cells, hop * cells)
        landing = own + either(side, -cells, cells)
        via = cells + 2 * reaches[l] + hop * cells
        straight, round_corner = either(side, east, west), either(side, next_row, last_row)
        return pltpu.make_async_remote_copy(
            src_ref=buf.at[pl.ds(own, count)],
            dst_ref=buf.at[pl.ds(either(turn, via, landing), count)],
            send_sem=hop_send.at[2 * slot + side],
            recv_sem=hop_recv.at[
                either(turn, 6 * layers * chunks + slot, 2 * slot + side)
            ],
            device_id={"lon": either(turn, round_corner, straight)},
            device_id_type=MESH,
        )

    def turned_copy(l, c, hop):
        count, buf = hop_cells(reaches[l], cells)[hop], zonal[l][c]
        slot = slot_of(l, c, hop)
        via = cells + 2 * reaches[l] + hop * cells
        landing = reaches[l] + either(turns_east, -count - hop * cells, (hop + 1) * cells)
        return pltpu.make_async_remote_copy(
            src_ref=buf.at[pl.ds(via, count)],
            dst_ref=buf.at[pl.ds(landing, count)],
            send_sem=via_send.at[slot],
            recv_sem=hop_recv.at[2 * slot + turns_east],
            device_id={"lon": along(either(turns_east, 1 - RING, RING - 1))},
            device_id_type=MESH,
        )

    def start_hop(l, c, hop, side):
        copy = hop_copy(l, c, hop, side, either(side, turns_east, turns_west))
        copy.start()
        sent.append(copy)

    def arrive(l, c, hop, side):
        hop_copy(l, c, hop, side, 0).wait_recv()

    def turn_on(l, c, hop):
        @pl.when(turns_east + turns_west == 1)
        def _():
            hop_copy(l, c, hop, turns_east, 1).wait_recv()
            turned_copy(l, c, hop).start()

    lat_copies = {}

    def start_lat(l, c, result):
        for which, chunk, row, peer in (
            (0, 0, 0, south),
            (1, chunks - 1, ROWS - 1, north),
        ):
            if c == chunk:
                edge[l, which] = result[:, row, :].astype(jnp.bfloat16)
                copy = pltpu.make_async_remote_copy(
                    src_ref=edge.at[l, which],
                    dst_ref=halo.at[l, which],
                    send_sem=lat_send.at[2 * l + which],
                    recv_sem=lat_recv.at[2 * l + which],
                    device_id={"lat": peer},
                    device_id_type=MESH,
                )
                copy.start()
                lat_copies[l, which] = copy

    def halo_row(l, which, outside):
        lat_copies[l, which].wait_recv()
        row = halo[l, which].astype(jnp.float32)
        row = jnp.where(outside, jnp.zeros_like(row), row)
        return row.reshape(cells, 1, chans)

    def conv_grad(l, c):
        if c == order[0]:
            loads["w_out", l].wait()
        rows = pl.ds(c * ROWS, ROWS)
        low = grad[:, rows, :].reshape(cells * ROWS, chans).astype(jnp.bfloat16)
        act = against(low, w_out[l])
        steep = slope[l, :, rows, :].reshape(cells * ROWS, hidden_units)
        pre = (act * steep).astype(jnp.bfloat16)
        result = against(pre, w_in[l]).reshape(cells, ROWS, chans)
        zonal[l][c][pl.ds(reaches[l], cells)] = result.astype(jnp.bfloat16)
        for side in sides:
            start_hop(l, c, 0, side)
        start_lat(l, c, result)

    def field(l, c):
        return zonal[l][c][pl.ds(reaches[l], cells)].astype(jnp.float32)

    def tapped(l, c):
        taps = [taps_ref[t, l, :].reshape(1, 1, chans) for t in range(5)]
        offset = dilation_ref[l]
        reach = reaches[l]
        place = lax.broadcasted_iota(jnp.int32, (cells, ROWS, chans), 1)
        here = field(l, c)
        if c + 1 < chunks:
            after = field(l, c + 1)
        else:
            after = halo_row(l, 0, lat == lat_count - 1)
        if c > 0:
            before = field(l, c - 1)
        else:
            before = halo_row(l, 1, lat == 0)
        from_north = pltpu.roll(jnp.where(place == 0, after, here), ROWS - 1, 1)
        from_south = pltpu.roll(jnp.where(place == ROWS - 1, before, here), 1, 1)
        window = zonal[l][c]
        ahead = window[pl.ds(reach + offset, cells)].astype(jnp.float32)
        behind = window[pl.ds(reach - offset, cells)].astype(jnp.float32)
        both = (taps[0] * ahead + taps[2] * behind).astype(jnp.bfloat16)
        return (
            both.astype(jnp.float32)
            + taps[1] * here
            + (taps[3] * from_north + taps[4] * from_south)
        )

    for c in order:
        conv_grad(layers - 1, c)

    for l in reversed(range(layers)):
        last = hop_count(l) - 1
        pieces = list(range(PIECES)) if l > 0 else []
        steps = [(hop, c) for hop in range(last) for c in order]
        ends = [(last, c) for c in order]

        def pass_on(step, side):
            arrive(l, step[1], step[0], side)
            start_hop(l, step[1], step[0] + 1, side)

        for i, step in enumerate(steps + ends[:LAG]):
            if step[0] < last:
                pass_on(step, sides[0])
            turn_on(l, step[1], step[0])
            if 0 <= i - LAG < len(steps):
                pass_on(steps[i - LAG], sides[1])
            if pieces and i % 2 == 1:
                slope_piece(l - 1, pieces.pop(0))
        for piece in pieces:
            slope_piece(l - 1, piece)
        for i, c in enumerate(order):
            for side in sides:
                arrive(l, c, last, side)
            rows = pl.ds(c * ROWS, ROWS)
            total = grad[:, rows, :] + tapped(l, c)
            if l > 0:
                grad[:, rows, :] = total
                conv_grad(l - 1, c)
            else:
                out_ref[:, rows, :] = total.astype(jnp.bfloat16)
            if i + LAG < chunks:
                turn_on(l, order[i + LAG], last)

    for copy in sent:
        copy.wait_send()

    @pl.when(turns_east + turns_west == 1)
    def _():
        for l in range(layers):
            for c in range(chunks):
                for hop in range(hop_count(l)):
                    turned_copy(l, c, hop).wait_send()

    for copy in lat_copies.values():
        copy.wait_send()


def whole_block(dims, reaches, *operands):
    layers, cells, lats, chans, hidden_units, _, _ = dims
    chunks = lats // ROWS
    dec_rows, values = operands[1].shape
    bf16, f32 = jnp.bfloat16, jnp.float32
    anywhere = pl.BlockSpec(memory_space=pl.ANY)
    return pl.pallas_call(
        functools.partial(kernel, dims, reaches),
        out_shape=jax.ShapeDtypeStruct((cells, lats, chans), bf16),
        in_specs=[
            pl.BlockSpec(memory_space=pltpu.SMEM),
            anywhere,
            anywhere,
            anywhere,
            anywhere,
            anywhere,
            pl.BlockSpec(memory_space=pltpu.VMEM),
        ],
        out_specs=pl.BlockSpec(memory_space=pltpu.VMEM),
        scratch_shapes=[
            pltpu.VMEM(
                (cells + 2 * reaches[l] + cells * len(hop_cells(reaches[l], cells)), ROWS, chans),
                bf16,
            )
            for l in range(layers)
            for c in range(chunks)
        ]
        + [
            pltpu.VMEM((layers, 2, cells, chans), bf16),
            pltpu.VMEM((layers, 2, cells, chans), bf16),
            pltpu.VMEM((dec_rows, values), bf16),
            pltpu.VMEM((chans, values), bf16),
            pltpu.VMEM((layers, cells * lats, chans), bf16),
            pltpu.VMEM((layers, chans, hidden_units), bf16),
            pltpu.VMEM((layers, hidden_units, chans), bf16),
            pltpu.VMEM((layers, cells, lats, hidden_units), f32),
            pltpu.VMEM((cells, lats, chans), f32),
            pltpu.SemaphoreType.DMA((3 * layers + 1,)),
            pltpu.SemaphoreType.DMA((2,)),
            pltpu.SemaphoreType.DMA((6 * layers * chunks,)),
            pltpu.SemaphoreType.DMA((9 * layers * chunks,)),
            pltpu.SemaphoreType.DMA((3 * layers * chunks,)),
            pltpu.SemaphoreType.DMA((2 * layers,)),
            pltpu.SemaphoreType.DMA((2 * layers,)),
        ],
        compiler_params=pltpu.CompilerParams(
            collective_id=0, has_side_effects=True, vmem_limit_bytes=60 << 20
        ),
    )(*operands)


def solution(mesh):
    lon_count, lat_count = mesh.shape["lon"], mesh.shape["lat"]

    def per_device(dec_cot, saved_conv, dec_weight, w_in, w_out, conv_taps, dilation):
        _, layers, cells, lats, chans = saved_conv.shape
        hidden_units = w_in.shape[2]
        dims = (layers, cells, lats, chans, hidden_units, lon_count, lat_count)
        reaches = (3 * cells,) * layers
        out = whole_block(
            dims,
            reaches,
            dilation,
            dec_cot[0].reshape(cells * lats, -1),
            saved_conv[0].reshape(layers, cells * lats, chans),
            dec_weight,
            w_in,
            w_out,
            conv_taps.transpose(1, 0, 2),
        )
        return out[None]

    in_specs = (
        P("segment", "lon", "lat", None),
        P("segment", None, "lon", "lat", None),
        P(),
        P(),
        P(),
        P(),
        P(),
    )
    out_specs = P("segment", "lon", "lat", None)
    return jax.shard_map(
        per_device, mesh=mesh, in_specs=in_specs, out_specs=out_specs, check_vma=False
    )
```

```python
import functools

import jax
import jax.numpy as jnp
from jax import lax
from jax.experimental import pallas as pl
from jax.experimental.pallas import tpu as pltpu
from jax.sharding import PartitionSpec as P

MESH = pl.DeviceIdType.MESH
ROWS = 8
RING = 12
LAG = 3
LEAD = 2
PIECES = 2


def gelu_slope(hidden):
    normal_cdf = 0.5 * (1.0 + lax.erf(hidden * 0.7071067811865476))
    density = jnp.exp(-0.5 * hidden * hidden) * 0.3989422804014327
    return normal_cdf + hidden * density


def against(left, right):
    return lax.dot_general(
        left, right, (((1,), (1,)), ((), ())), preferred_element_type=jnp.float32
    )


def hop_cells(reach, cells):
    counts = []
    while reach > 0:
        counts.append(min(reach, cells))
        reach -= cells
    return counts


def kernel(
    dims,
    reaches,
    dilation_ref,
    dec_cot_ref,
    saved_ref,
    dec_weight_ref,
    w_in_ref,
    w_out_ref,
    taps_ref,
    out_ref,
    *scratch,
):
    layers, cells, lats, chans, hidden_units, lon_count, lat_count = dims
    chunks = lats // ROWS
    zonal = [scratch[l * chunks : (l + 1) * chunks] for l in range(layers)]
    (
        edge,
        halo,
        dec_here,
        dec_weight,
        saved,
        w_in,
        w_out,
        slope,
        grad,
        load_sem,
        dec_sem,
        hop_send,
        hop_recv,
        via_send,
        lat_send,
        lat_recv,
    ) = scratch[layers * chunks :]

    seg = lax.axis_index("segment")
    lon = lax.axis_index("lon")
    lat = lax.axis_index("lat")
    east = lax.rem(lon + 1, lon_count)
    west = lax.rem(lon + lon_count - 1, lon_count)
    north = lax.rem(lat + 1, lat_count)
    south = lax.rem(lat + lat_count - 1, lat_count)

    def along(steps):
        return lax.rem(lon + lon_count + steps, lon_count)

    place_in_row = lax.rem(lon, RING)
    turns = lat // (lat_count // 2)
    turns_east = turns * (place_in_row // (RING - 1))
    turns_west = turns * ((RING - 1 - place_in_row) // (RING - 1))
    at_end = place_in_row // (RING - 1) + (RING - 1 - place_in_row) // (RING - 1)
    next_row, last_row = along(RING), along(-RING)

    barrier = pltpu.get_barrier_semaphore()
    for peer in (
        {"segment": 1 - seg},
        {"lon": east},
        {"lon": west},
        {"lat": north},
        {"lat": south},
        {"lon": next_row},
        {"lon": last_row},
        {"lon": along(RING - 1)},
        {"lon": along(1 - RING)},
    ):
        pl.semaphore_signal(barrier, inc=1, device_id=peer, device_id_type=MESH)

    loads = {}

    def load(name, src, dst):
        loads[name] = pltpu.make_async_copy(src, dst, load_sem.at[len(loads)])
        loads[name].start()

    for l in reversed(range(layers)):
        load(("saved", l), saved_ref.at[l], saved.at[l])
        load(("w_in", l), w_in_ref.at[l], w_in.at[l])
        if l == layers - 1:
            load("dec_weight", dec_weight_ref, dec_weight)
        load(("w_out", l), w_out_ref.at[l], w_out.at[l])

    def slope_piece(l, piece):
        if piece == 0:
            loads["saved", l].wait()
            loads["w_in", l].wait()
        span = cells // PIECES
        rows = span * lats
        hidden = jnp.dot(
            saved[l, pl.ds(piece * rows, rows), :],
            w_in[l],
            preferred_element_type=jnp.float32,
        )
        slope[l, pl.ds(piece * span, span)] = gelu_slope(hidden).reshape(
            span, lats, hidden_units
        )

    pl.semaphore_wait(barrier, 9)
    dec_copy = pltpu.make_async_remote_copy(
        src_ref=dec_cot_ref,
        dst_ref=dec_here,
        send_sem=dec_sem.at[0],
        recv_sem=dec_sem.at[1],
        device_id={"segment": 1 - seg},
        device_id_type=MESH,
    )
    dec_copy.start()
    for piece in range(PIECES):
        slope_piece(layers - 1, piece)
    loads["dec_weight"].wait()
    dec_copy.wait()
    handed = against(dec_here[...], dec_weight[...]).astype(jnp.bfloat16)
    grad[...] = handed.astype(jnp.float32).reshape(cells, lats, chans)

    order = [c for c in range(chunks) if 0 < c < chunks - 1] + [chunks - 1, 0]
    quick = place_in_row // (RING // 2)
    sides = (quick, 1 - quick)

    def hop_count(l):
        return len(hop_cells(reaches[l], cells))

    def slot_of(l, c, hop):
        return (l * chunks + c) * 3 + hop

    def either(choice, one, other):
        return other + choice * (one - other)

    def hop_copy(l, c, hop, side, turn):
        count, buf = hop_cells(reaches[l], cells)[hop], zonal[l][c]
        slot = slot_of(l, c, hop)
        own = reaches[l] + either(side, cells - count - hop * cells, hop * cells)
        landing = own + either(side, -cells, cells)
        via = cells + 2 * reaches[l] + hop * cells
        straight, round_corner = either(side, east, west), either(side, next_row, last_row)
        return pltpu.make_async_remote_copy(
            src_ref=buf.at[pl.ds(own, count)],
            dst_ref=buf.at[pl.ds(either(turn, via, landing), count)],
            send_sem=hop_send.at[2 * slot + side],
            recv_sem=hop_recv.at[
                either(turn, 6 * layers * chunks + slot, 2 * slot + side)
            ],
            device_id={"lon": either(turn, round_corner, straight)},
            device_id_type=MESH,
        )

    def turned_copy(l, c, hop):
        count, buf = hop_cells(reaches[l], cells)[hop], zonal[l][c]
        slot = slot_of(l, c, hop)
        via = cells + 2 * reaches[l] + hop * cells
        landing = reaches[l] + either(turns_east, -count - hop * cells, (hop + 1) * cells)
        return pltpu.make_async_remote_copy(
            src_ref=buf.at[pl.ds(via, count)],
            dst_ref=buf.at[pl.ds(landing, count)],
            send_sem=via_send.at[slot],
            recv_sem=hop_recv.at[2 * slot + turns_east],
            device_id={"lon": along(either(turns_east, 1 - RING, RING - 1))},
            device_id_type=MESH,
        )

    def start_hop(l, c, hop, side):
        hop_copy(l, c, hop, side, either(side, turns_east, turns_west)).start()

    def arrive(l, c, hop, side):
        hop_copy(l, c, hop, side, 0).wait_recv()

    def turn_on(l, c, hop):
        @pl.when(turns_east + turns_west == 1)
        def _():
            hop_copy(l, c, hop, turns_east, 1).wait_recv()
            turned_copy(l, c, hop).start()

    lat_copies = {}

    def start_lat(l, c, result):
        for which, chunk, row, peer in (
            (0, 0, 0, south),
            (1, chunks - 1, ROWS - 1, north),
        ):
            if c == chunk:
                edge[l, which] = result[:, row, :].astype(jnp.bfloat16)
                copy = pltpu.make_async_remote_copy(
                    src_ref=edge.at[l, which],
                    dst_ref=halo.at[l, which],
                    send_sem=lat_send.at[2 * l + which],
                    recv_sem=lat_recv.at[2 * l + which],
                    device_id={"lat": peer},
                    device_id_type=MESH,
                )
                copy.start()
                lat_copies[l, which] = copy

    def halo_row(l, which, outside):
        lat_copies[l, which].wait_recv()
        row = halo[l, which].astype(jnp.float32)
        row = jnp.where(outside, jnp.zeros_like(row), row)
        return row.reshape(cells, 1, chans)

    def conv_grad(l, c):
        if c == order[0]:
            loads["w_out", l].wait()
        rows = pl.ds(c * ROWS, ROWS)
        low = grad[:, rows, :].reshape(cells * ROWS, chans).astype(jnp.bfloat16)
        act = against(low, w_out[l])
        steep = slope[l, :, rows, :].reshape(cells * ROWS, hidden_units)
        pre = (act * steep).astype(jnp.bfloat16)
        result = against(pre, w_in[l]).reshape(cells, ROWS, chans)
        zonal[l][c][pl.ds(reaches[l], cells)] = result.astype(jnp.bfloat16)
        for side in sides:
            start_hop(l, c, 0, side)
        start_lat(l, c, result)

    def field(l, c):
        return zonal[l][c][pl.ds(reaches[l], cells)].astype(jnp.float32)

    def tapped(l, c):
        taps = [taps_ref[t, l, :].reshape(1, 1, chans) for t in range(5)]
        offset = dilation_ref[l]
        reach = reaches[l]
        place = lax.broadcasted_iota(jnp.int32, (cells, ROWS, chans), 1)
        here = field(l, c)
        if c + 1 < chunks:
            after = field(l, c + 1)
        else:
            after = halo_row(l, 0, lat == lat_count - 1)
        if c > 0:
            before = field(l, c - 1)
        else:
            before = halo_row(l, 1, lat == 0)
        from_north = pltpu.roll(jnp.where(place == 0, after, here), ROWS - 1, 1)
        from_south = pltpu.roll(jnp.where(place == ROWS - 1, before, here), 1, 1)
        window = zonal[l][c]
        ahead = window[pl.ds(reach + offset, cells)].astype(jnp.float32)
        behind = window[pl.ds(reach - offset, cells)].astype(jnp.float32)
        both = (taps[0] * ahead + taps[2] * behind).astype(jnp.bfloat16)
        return (
            both.astype(jnp.float32)
            + taps[1] * here
            + (taps[3] * from_north + taps[4] * from_south)
        )

    for c in order:
        conv_grad(layers - 1, c)

    for l in reversed(range(layers)):
        last = hop_count(l) - 1
        pieces = list(range(PIECES)) if l > 0 else []
        steps = [(hop, c) for hop in range(last) for c in order]
        ends = [(last, c) for c in order]

        def pass_on(step, side):
            arrive(l, step[1], step[0], side)
            start_hop(l, step[1], step[0] + 1, side)

        for piece in pieces:
            slope_piece(l - 1, piece)
        events = list(enumerate(steps + ends[:LEAD] + [None] * LAG))

        def relay(lag):
            for i, step in events:
                if step is not None:
                    if step[0] < last:
                        pass_on(step, sides[0])
                    turn_on(l, step[1], step[0])
                if 0 <= i - lag < len(steps):
                    pass_on(steps[i - lag], sides[1])

        pl.when(at_end == 1)(functools.partial(relay, LAG))
        pl.when(at_end == 0)(functools.partial(relay, 0))
        for i, c in enumerate(order):
            for side in sides:
                arrive(l, c, last, side)
            rows = pl.ds(c * ROWS, ROWS)
            total = grad[:, rows, :] + tapped(l, c)
            if l > 0:
                grad[:, rows, :] = total
                conv_grad(l - 1, c)
            else:
                out_ref[:, rows, :] = total.astype(jnp.bfloat16)
            if i + LEAD < chunks:
                turn_on(l, order[i + LEAD], last)

    for l in range(layers):
        for c in range(chunks):
            for hop in range(hop_count(l)):
                for side in range(2):
                    hop_copy(l, c, hop, side, 0).wait_send()

    @pl.when(turns_east + turns_west == 1)
    def _():
        for l in range(layers):
            for c in range(chunks):
                for hop in range(hop_count(l)):
                    turned_copy(l, c, hop).wait_send()

    for copy in lat_copies.values():
        copy.wait_send()


def whole_block(dims, reaches, *operands):
    layers, cells, lats, chans, hidden_units, _, _ = dims
    chunks = lats // ROWS
    dec_rows, values = operands[1].shape
    bf16, f32 = jnp.bfloat16, jnp.float32
    anywhere = pl.BlockSpec(memory_space=pl.ANY)
    return pl.pallas_call(
        functools.partial(kernel, dims, reaches),
        out_shape=jax.ShapeDtypeStruct((cells, lats, chans), bf16),
        in_specs=[
            pl.BlockSpec(memory_space=pltpu.SMEM),
            anywhere,
            anywhere,
            anywhere,
            anywhere,
            anywhere,
            pl.BlockSpec(memory_space=pltpu.VMEM),
        ],
        out_specs=pl.BlockSpec(memory_space=pltpu.VMEM),
        scratch_shapes=[
            pltpu.VMEM(
                (cells + 2 * reaches[l] + cells * len(hop_cells(reaches[l], cells)), ROWS, chans),
                bf16,
            )
            for l in range(layers)
            for c in range(chunks)
        ]
        + [
            pltpu.VMEM((layers, 2, cells, chans), bf16),
            pltpu.VMEM((layers, 2, cells, chans), bf16),
            pltpu.VMEM((dec_rows, values), bf16),
            pltpu.VMEM((chans, values), bf16),
            pltpu.VMEM((layers, cells * lats, chans), bf16),
            pltpu.VMEM((layers, chans, hidden_units), bf16),
            pltpu.VMEM((layers, hidden_units, chans), bf16),
            pltpu.VMEM((layers, cells, lats, hidden_units), f32),
            pltpu.VMEM((cells, lats, chans), f32),
            pltpu.SemaphoreType.DMA((3 * layers + 1,)),
            pltpu.SemaphoreType.DMA((2,)),
            pltpu.SemaphoreType.DMA((6 * layers * chunks,)),
            pltpu.SemaphoreType.DMA((9 * layers * chunks,)),
            pltpu.SemaphoreType.DMA((3 * layers * chunks,)),
            pltpu.SemaphoreType.DMA((2 * layers,)),
            pltpu.SemaphoreType.DMA((2 * layers,)),
        ],
        compiler_params=pltpu.CompilerParams(
            collective_id=0, has_side_effects=True, vmem_limit_bytes=60 << 20
        ),
    )(*operands)


def solution(mesh):
    lon_count, lat_count = mesh.shape["lon"], mesh.shape["lat"]

    def per_device(dec_cot, saved_conv, dec_weight, w_in, w_out, conv_taps, dilation):
        _, layers, cells, lats, chans = saved_conv.shape
        hidden_units = w_in.shape[2]
        dims = (layers, cells, lats, chans, hidden_units, lon_count, lat_count)
        reaches = (3 * cells,) * layers
        out = whole_block(
            dims,
            reaches,
            dilation,
            dec_cot[0].reshape(cells * lats, -1),
            saved_conv[0].reshape(layers, cells * lats, chans),
            dec_weight,
            w_in,
            w_out,
            conv_taps.transpose(1, 0, 2),
        )
        return out[None]

    in_specs = (
        P("segment", "lon", "lat", None),
        P("segment", None, "lon", "lat", None),
        P(),
        P(),
        P(),
        P(),
        P(),
    )
    out_specs = P("segment", "lon", "lat", None)
    return jax.shard_map(
        per_device, mesh=mesh, in_specs=in_specs, out_specs=out_specs, check_vma=False
    )
```

```python
import functools

import jax
import jax.numpy as jnp
from jax import lax
from jax.experimental import pallas as pl
from jax.experimental.pallas import tpu as pltpu
from jax.sharding import PartitionSpec as P

MESH = pl.DeviceIdType.MESH
ROWS = 8
RING = 12
LAG = 4
LEAD = 2
PIECES = 2


def gelu_slope(hidden):
    normal_cdf = 0.5 * (1.0 + lax.erf(hidden * 0.7071067811865476))
    density = jnp.exp(-0.5 * hidden * hidden) * 0.3989422804014327
    return normal_cdf + hidden * density


def against(left, right):
    return lax.dot_general(
        left, right, (((1,), (1,)), ((), ())), preferred_element_type=jnp.float32
    )


def hop_cells(reach, cells):
    counts = []
    while reach > 0:
        counts.append(min(reach, cells))
        reach -= cells
    return counts


def kernel(
    dims,
    reaches,
    dilation_ref,
    dec_cot_ref,
    saved_ref,
    dec_weight_ref,
    w_in_ref,
    w_out_ref,
    taps_ref,
    out_ref,
    *scratch,
):
    layers, cells, lats, chans, hidden_units, lon_count, lat_count = dims
    chunks = lats // ROWS
    zonal = [scratch[l * chunks : (l + 1) * chunks] for l in range(layers)]
    (
        edge,
        halo,
        dec_here,
        dec_weight,
        saved,
        w_in,
        w_out,
        slope,
        grad,
        load_sem,
        dec_sem,
        hop_send,
        hop_recv,
        via_send,
        lat_send,
        lat_recv,
    ) = scratch[layers * chunks :]

    seg = lax.axis_index("segment")
    lon = lax.axis_index("lon")
    lat = lax.axis_index("lat")
    east = lax.rem(lon + 1, lon_count)
    west = lax.rem(lon + lon_count - 1, lon_count)
    north = lax.rem(lat + 1, lat_count)
    south = lax.rem(lat + lat_count - 1, lat_count)

    def along(steps):
        return lax.rem(lon + lon_count + steps, lon_count)

    place_in_row = lax.rem(lon, RING)
    turns = seg
    turns_east = turns * (place_in_row // (RING - 1))
    turns_west = turns * ((RING - 1 - place_in_row) // (RING - 1))
    at_end = place_in_row // (RING - 1) + (RING - 1 - place_in_row) // (RING - 1)
    next_row, last_row = along(RING), along(-RING)

    barrier = pltpu.get_barrier_semaphore()
    for peer in (
        {"segment": 1 - seg},
        {"lon": east},
        {"lon": west},
        {"lat": north},
        {"lat": south},
        {"lon": next_row},
        {"lon": last_row},
        {"lon": along(RING - 1)},
        {"lon": along(1 - RING)},
    ):
        pl.semaphore_signal(barrier, inc=1, device_id=peer, device_id_type=MESH)

    loads = {}

    def load(name, src, dst):
        loads[name] = pltpu.make_async_copy(src, dst, load_sem.at[len(loads)])
        loads[name].start()

    for l in reversed(range(layers)):
        load(("saved", l), saved_ref.at[l], saved.at[l])
        load(("w_in", l), w_in_ref.at[l], w_in.at[l])
        if l == layers - 1:
            load("dec_weight", dec_weight_ref, dec_weight)
        load(("w_out", l), w_out_ref.at[l], w_out.at[l])

    def slope_piece(l, piece):
        if piece == 0:
            loads["saved", l].wait()
            loads["w_in", l].wait()
        span = cells // PIECES
        rows = span * lats
        hidden = jnp.dot(
            saved[l, pl.ds(piece * rows, rows), :],
            w_in[l],
            preferred_element_type=jnp.float32,
        )
        slope[l, pl.ds(piece * span, span)] = gelu_slope(hidden).reshape(
            span, lats, hidden_units
        )

    pl.semaphore_wait(barrier, 9)
    dec_copy = pltpu.make_async_remote_copy(
        src_ref=dec_cot_ref,
        dst_ref=dec_here,
        send_sem=dec_sem.at[0],
        recv_sem=dec_sem.at[1],
        device_id={"segment": 1 - seg},
        device_id_type=MESH,
    )
    dec_copy.start()
    for piece in range(PIECES):
        slope_piece(layers - 1, piece)
    loads["dec_weight"].wait()
    dec_copy.wait()
    handed = against(dec_here[...], dec_weight[...]).astype(jnp.bfloat16)
    grad[...] = handed.astype(jnp.float32).reshape(cells, lats, chans)

    order = [c for c in range(chunks) if 0 < c < chunks - 1] + [chunks - 1, 0]
    quick = place_in_row // (RING // 2)
    sides = (quick, 1 - quick)

    def hop_count(l):
        return len(hop_cells(reaches[l], cells))

    def slot_of(l, c, hop):
        return (l * chunks + c) * 3 + hop

    def either(choice, one, other):
        return other + choice * (one - other)

    def hop_copy(l, c, hop, side, turn):
        count, buf = hop_cells(reaches[l], cells)[hop], zonal[l][c]
        slot = slot_of(l, c, hop)
        own = reaches[l] + either(side, cells - count - hop * cells, hop * cells)
        landing = own + either(side, -cells, cells)
        via = cells + 2 * reaches[l] + hop * cells
        straight, round_corner = either(side, east, west), either(side, next_row, last_row)
        return pltpu.make_async_remote_copy(
            src_ref=buf.at[pl.ds(own, count)],
            dst_ref=buf.at[pl.ds(either(turn, via, landing), count)],
            send_sem=hop_send.at[2 * slot + side],
            recv_sem=hop_recv.at[
                either(turn, 6 * layers * chunks + slot, 2 * slot + side)
            ],
            device_id={"lon": either(turn, round_corner, straight)},
            device_id_type=MESH,
        )

    def turned_copy(l, c, hop):
        count, buf = hop_cells(reaches[l], cells)[hop], zonal[l][c]
        slot = slot_of(l, c, hop)
        via = cells + 2 * reaches[l] + hop * cells
        landing = reaches[l] + either(turns_east, -count - hop * cells, (hop + 1) * cells)
        return pltpu.make_async_remote_copy(
            src_ref=buf.at[pl.ds(via, count)],
            dst_ref=buf.at[pl.ds(landing, count)],
            send_sem=via_send.at[slot],
            recv_sem=hop_recv.at[2 * slot + turns_east],
            device_id={"lon": along(either(turns_east, 1 - RING, RING - 1))},
            device_id_type=MESH,
        )

    def start_hop(l, c, hop, side):
        hop_copy(l, c, hop, side, either(side, turns_east, turns_west)).start()

    def arrive(l, c, hop, side):
        hop_copy(l, c, hop, side, 0).wait_recv()

    def turn_on(l, c, hop):
        @pl.when(turns_east + turns_west == 1)
        def _():
            hop_copy(l, c, hop, turns_east, 1).wait_recv()
            turned_copy(l, c, hop).start()

    lat_copies = {}

    def start_lat(l, c, result):
        for which, chunk, row, peer in (
            (0, 0, 0, south),
            (1, chunks - 1, ROWS - 1, north),
        ):
            if c == chunk:
                edge[l, which] = result[:, row, :].astype(jnp.bfloat16)
                copy = pltpu.make_async_remote_copy(
                    src_ref=edge.at[l, which],
                    dst_ref=halo.at[l, which],
                    send_sem=lat_send.at[2 * l + which],
                    recv_sem=lat_recv.at[2 * l + which],
                    device_id={"lat": peer},
                    device_id_type=MESH,
                )
                copy.start()
                lat_copies[l, which] = copy

    def halo_row(l, which, outside):
        lat_copies[l, which].wait_recv()
        row = halo[l, which].astype(jnp.float32)
        row = jnp.where(outside, jnp.zeros_like(row), row)
        return row.reshape(cells, 1, chans)

    def conv_grad(l, c):
        if c == order[0]:
            loads["w_out", l].wait()
        rows = pl.ds(c * ROWS, ROWS)
        low = grad[:, rows, :].reshape(cells * ROWS, chans).astype(jnp.bfloat16)
        act = against(low, w_out[l])
        steep = slope[l, :, rows, :].reshape(cells * ROWS, hidden_units)
        pre = (act * steep).astype(jnp.bfloat16)
        result = against(pre, w_in[l]).reshape(cells, ROWS, chans)
        zonal[l][c][pl.ds(reaches[l], cells)] = result.astype(jnp.bfloat16)
        for side in sides:
            start_hop(l, c, 0, side)
        start_lat(l, c, result)

    def field(l, c):
        return zonal[l][c][pl.ds(reaches[l], cells)].astype(jnp.float32)

    def tapped(l, c):
        taps = [taps_ref[t, l, :].reshape(1, 1, chans) for t in range(5)]
        offset = dilation_ref[l]
        reach = reaches[l]
        place = lax.broadcasted_iota(jnp.int32, (cells, ROWS, chans), 1)
        here = field(l, c)
        if c + 1 < chunks:
            after = field(l, c + 1)
        else:
            after = halo_row(l, 0, lat == lat_count - 1)
        if c > 0:
            before = field(l, c - 1)
        else:
            before = halo_row(l, 1, lat == 0)
        from_north = pltpu.roll(jnp.where(place == 0, after, here), ROWS - 1, 1)
        from_south = pltpu.roll(jnp.where(place == ROWS - 1, before, here), 1, 1)
        window = zonal[l][c]
        ahead = window[pl.ds(reach + offset, cells)].astype(jnp.float32)
        behind = window[pl.ds(reach - offset, cells)].astype(jnp.float32)
        both = (taps[0] * ahead + taps[2] * behind).astype(jnp.bfloat16)
        return (
            both.astype(jnp.float32)
            + taps[1] * here
            + (taps[3] * from_north + taps[4] * from_south)
        )

    for c in order:
        conv_grad(layers - 1, c)

    for l in reversed(range(layers)):
        last = hop_count(l) - 1
        pieces = list(range(PIECES)) if l > 0 else []
        steps = [(hop, c) for hop in range(last) for c in order]
        ends = [(last, c) for c in order]

        def pass_on(step, side):
            arrive(l, step[1], step[0], side)
            start_hop(l, step[1], step[0] + 1, side)

        for piece in pieces:
            slope_piece(l - 1, piece)
        events = list(enumerate(steps + ends[:LEAD] + [None] * LAG))

        def relay(lag):
            for i, step in events:
                if step is not None:
                    if step[0] < last:
                        pass_on(step, sides[0])
                    turn_on(l, step[1], step[0])
                if 0 <= i - lag < len(steps):
                    pass_on(steps[i - lag], sides[1])

        pl.when(at_end == 1)(functools.partial(relay, LAG))
        pl.when(at_end == 0)(functools.partial(relay, 0))
        for i, c in enumerate(order):
            for side in sides:
                arrive(l, c, last, side)
            rows = pl.ds(c * ROWS, ROWS)
            total = grad[:, rows, :] + tapped(l, c)
            if l > 0:
                grad[:, rows, :] = total
                conv_grad(l - 1, c)
            else:
                out_ref[:, rows, :] = total.astype(jnp.bfloat16)
            if i + LEAD < chunks:
                turn_on(l, order[i + LEAD], last)

    for l in range(layers):
        for c in range(chunks):
            for hop in range(hop_count(l)):
                for side in range(2):
                    hop_copy(l, c, hop, side, 0).wait_send()

    @pl.when(turns_east + turns_west == 1)
    def _():
        for l in range(layers):
            for c in range(chunks):
                for hop in range(hop_count(l)):
                    turned_copy(l, c, hop).wait_send()

    for copy in lat_copies.values():
        copy.wait_send()


def whole_block(dims, reaches, *operands):
    layers, cells, lats, chans, hidden_units, _, _ = dims
    chunks = lats // ROWS
    dec_rows, values = operands[1].shape
    bf16, f32 = jnp.bfloat16, jnp.float32
    anywhere = pl.BlockSpec(memory_space=pl.ANY)
    return pl.pallas_call(
        functools.partial(kernel, dims, reaches),
        out_shape=jax.ShapeDtypeStruct((cells, lats, chans), bf16),
        in_specs=[
            pl.BlockSpec(memory_space=pltpu.SMEM),
            anywhere,
            anywhere,
            anywhere,
            anywhere,
            anywhere,
            pl.BlockSpec(memory_space=pltpu.VMEM),
        ],
        out_specs=pl.BlockSpec(memory_space=pltpu.VMEM),
        scratch_shapes=[
            pltpu.VMEM(
                (cells + 2 * reaches[l] + cells * len(hop_cells(reaches[l], cells)), ROWS, chans),
                bf16,
            )
            for l in range(layers)
            for c in range(chunks)
        ]
        + [
            pltpu.VMEM((layers, 2, cells, chans), bf16),
            pltpu.VMEM((layers, 2, cells, chans), bf16),
            pltpu.VMEM((dec_rows, values), bf16),
            pltpu.VMEM((chans, values), bf16),
            pltpu.VMEM((layers, cells * lats, chans), bf16),
            pltpu.VMEM((layers, chans, hidden_units), bf16),
            pltpu.VMEM((layers, hidden_units, chans), bf16),
            pltpu.VMEM((layers, cells, lats, hidden_units), f32),
            pltpu.VMEM((cells, lats, chans), f32),
            pltpu.SemaphoreType.DMA((3 * layers + 1,)),
            pltpu.SemaphoreType.DMA((2,)),
            pltpu.SemaphoreType.DMA((6 * layers * chunks,)),
            pltpu.SemaphoreType.DMA((9 * layers * chunks,)),
            pltpu.SemaphoreType.DMA((3 * layers * chunks,)),
            pltpu.SemaphoreType.DMA((2 * layers,)),
            pltpu.SemaphoreType.DMA((2 * layers,)),
        ],
        compiler_params=pltpu.CompilerParams(
            collective_id=0, has_side_effects=True, vmem_limit_bytes=60 << 20
        ),
    )(*operands)


def solution(mesh):
    lon_count, lat_count = mesh.shape["lon"], mesh.shape["lat"]

    def per_device(dec_cot, saved_conv, dec_weight, w_in, w_out, conv_taps, dilation):
        _, layers, cells, lats, chans = saved_conv.shape
        hidden_units = w_in.shape[2]
        dims = (layers, cells, lats, chans, hidden_units, lon_count, lat_count)
        reaches = (3 * cells,) * layers
        out = whole_block(
            dims,
            reaches,
            dilation,
            dec_cot[0].reshape(cells * lats, -1),
            saved_conv[0].reshape(layers, cells * lats, chans),
            dec_weight,
            w_in,
            w_out,
            conv_taps.transpose(1, 0, 2),
        )
        return out[None]

    in_specs = (
        P("segment", "lon", "lat", None),
        P("segment", None, "lon", "lat", None),
        P(),
        P(),
        P(),
        P(),
        P(),
    )
    out_specs = P("segment", "lon", "lat", None)
    return jax.shard_map(
        per_device, mesh=mesh, in_specs=in_specs, out_specs=out_specs, check_vma=False
    )
```

```python
import functools

import jax
import jax.numpy as jnp
from jax import lax
from jax.experimental import pallas as pl
from jax.experimental.pallas import tpu as pltpu
from jax.sharding import PartitionSpec as P

MESH = pl.DeviceIdType.MESH
ROWS = 8
RING = 12
LAG = 5
LEAD = 2
PIECES = 2


def gelu_slope(hidden):
    normal_cdf = 0.5 * (1.0 + lax.erf(hidden * 0.7071067811865476))
    density = jnp.exp(-0.5 * hidden * hidden) * 0.3989422804014327
    return normal_cdf + hidden * density


def against(left, right):
    return lax.dot_general(
        left, right, (((1,), (1,)), ((), ())), preferred_element_type=jnp.float32
    )


def hop_cells(reach, cells):
    counts = []
    while reach > 0:
        counts.append(min(reach, cells))
        reach -= cells
    return counts


def kernel(
    dims,
    reaches,
    dilation_ref,
    dec_cot_ref,
    saved_ref,
    dec_weight_ref,
    w_in_ref,
    w_out_ref,
    taps_ref,
    out_ref,
    *scratch,
):
    layers, cells, lats, chans, hidden_units, lon_count, lat_count = dims
    chunks = lats // ROWS
    zonal = [scratch[l * chunks : (l + 1) * chunks] for l in range(layers)]
    (
        edge,
        halo,
        dec_here,
        dec_weight,
        saved,
        w_in,
        w_out,
        slope,
        grad,
        load_sem,
        dec_sem,
        hop_send,
        hop_recv,
        via_send,
        lat_send,
        lat_recv,
    ) = scratch[layers * chunks :]

    seg = lax.axis_index("segment")
    lon = lax.axis_index("lon")
    lat = lax.axis_index("lat")
    east = lax.rem(lon + 1, lon_count)
    west = lax.rem(lon + lon_count - 1, lon_count)
    north = lax.rem(lat + 1, lat_count)
    south = lax.rem(lat + lat_count - 1, lat_count)

    def along(steps):
        return lax.rem(lon + lon_count + steps, lon_count)

    place_in_row = lax.rem(lon, RING)
    turns = seg
    turns_east = turns * (place_in_row // (RING - 1))
    turns_west = turns * ((RING - 1 - place_in_row) // (RING - 1))
    at_end = place_in_row // (RING - 1) + (RING - 1 - place_in_row) // (RING - 1)
    next_row, last_row = along(RING), along(-RING)

    barrier = pltpu.get_barrier_semaphore()
    for peer in (
        {"segment": 1 - seg},
        {"lon": east},
        {"lon": west},
        {"lat": north},
        {"lat": south},
        {"lon": next_row},
        {"lon": last_row},
        {"lon": along(RING - 1)},
        {"lon": along(1 - RING)},
    ):
        pl.semaphore_signal(barrier, inc=1, device_id=peer, device_id_type=MESH)

    loads = {}

    def load(name, src, dst):
        loads[name] = pltpu.make_async_copy(src, dst, load_sem.at[len(loads)])
        loads[name].start()

    for l in reversed(range(layers)):
        load(("saved", l), saved_ref.at[l], saved.at[l])
        load(("w_in", l), w_in_ref.at[l], w_in.at[l])
        if l == layers - 1:
            load("dec_weight", dec_weight_ref, dec_weight)
        load(("w_out", l), w_out_ref.at[l], w_out.at[l])

    def slope_piece(l, piece):
        if piece == 0:
            loads["saved", l].wait()
            loads["w_in", l].wait()
        span = cells // PIECES
        rows = span * lats
        hidden = jnp.dot(
            saved[l, pl.ds(piece * rows, rows), :],
            w_in[l],
            preferred_element_type=jnp.float32,
        )
        slope[l, pl.ds(piece * span, span)] = gelu_slope(hidden).reshape(
            span, lats, hidden_units
        )

    pl.semaphore_wait(barrier, 9)
    dec_copy = pltpu.make_async_remote_copy(
        src_ref=dec_cot_ref,
        dst_ref=dec_here,
        send_sem=dec_sem.at[0],
        recv_sem=dec_sem.at[1],
        device_id={"segment": 1 - seg},
        device_id_type=MESH,
    )
    dec_copy.start()
    for piece in range(PIECES):
        slope_piece(layers - 1, piece)
    loads["dec_weight"].wait()
    dec_copy.wait()
    handed = against(dec_here[...], dec_weight[...]).astype(jnp.bfloat16)
    grad[...] = handed.astype(jnp.float32).reshape(cells, lats, chans)

    order = [c for c in range(chunks) if 0 < c < chunks - 1] + [chunks - 1, 0]
    quick = place_in_row // (RING // 2)
    sides = (quick, 1 - quick)

    def hop_count(l):
        return len(hop_cells(reaches[l], cells))

    def slot_of(l, c, hop):
        return (l * chunks + c) * 3 + hop

    def either(choice, one, other):
        return other + choice * (one - other)

    def hop_copy(l, c, hop, side, turn):
        count, buf = hop_cells(reaches[l], cells)[hop], zonal[l][c]
        slot = slot_of(l, c, hop)
        own = reaches[l] + either(side, cells - count - hop * cells, hop * cells)
        landing = own + either(side, -cells, cells)
        via = cells + 2 * reaches[l] + hop * cells
        straight, round_corner = either(side, east, west), either(side, next_row, last_row)
        return pltpu.make_async_remote_copy(
            src_ref=buf.at[pl.ds(own, count)],
            dst_ref=buf.at[pl.ds(either(turn, via, landing), count)],
            send_sem=hop_send.at[2 * slot + side],
            recv_sem=hop_recv.at[
                either(turn, 6 * layers * chunks + slot, 2 * slot + side)
            ],
            device_id={"lon": either(turn, round_corner, straight)},
            device_id_type=MESH,
        )

    def turned_copy(l, c, hop):
        count, buf = hop_cells(reaches[l], cells)[hop], zonal[l][c]
        slot = slot_of(l, c, hop)
        via = cells + 2 * reaches[l] + hop * cells
        landing = reaches[l] + either(turns_east, -count - hop * cells, (hop + 1) * cells)
        return pltpu.make_async_remote_copy(
            src_ref=buf.at[pl.ds(via, count)],
            dst_ref=buf.at[pl.ds(landing, count)],
            send_sem=via_send.at[slot],
            recv_sem=hop_recv.at[2 * slot + turns_east],
            device_id={"lon": along(either(turns_east, 1 - RING, RING - 1))},
            device_id_type=MESH,
        )

    def start_hop(l, c, hop, side):
        hop_copy(l, c, hop, side, either(side, turns_east, turns_west)).start()

    def arrive(l, c, hop, side):
        hop_copy(l, c, hop, side, 0).wait_recv()

    def turn_on(l, c, hop):
        @pl.when(turns_east + turns_west == 1)
        def _():
            hop_copy(l, c, hop, turns_east, 1).wait_recv()
            turned_copy(l, c, hop).start()

    lat_copies = {}

    def start_lat(l, c, result):
        for which, chunk, row, peer in (
            (0, 0, 0, south),
            (1, chunks - 1, ROWS - 1, north),
        ):
            if c == chunk:
                edge[l, which] = result[:, row, :].astype(jnp.bfloat16)
                copy = pltpu.make_async_remote_copy(
                    src_ref=edge.at[l, which],
                    dst_ref=halo.at[l, which],
                    send_sem=lat_send.at[2 * l + which],
                    recv_sem=lat_recv.at[2 * l + which],
                    device_id={"lat": peer},
                    device_id_type=MESH,
                )
                copy.start()
                lat_copies[l, which] = copy

    def halo_row(l, which, outside):
        lat_copies[l, which].wait_recv()
        row = halo[l, which].astype(jnp.float32)
        row = jnp.where(outside, jnp.zeros_like(row), row)
        return row.reshape(cells, 1, chans)

    def conv_grad(l, c):
        if c == order[0]:
            loads["w_out", l].wait()
        rows = pl.ds(c * ROWS, ROWS)
        low = grad[:, rows, :].reshape(cells * ROWS, chans).astype(jnp.bfloat16)
        act = against(low, w_out[l])
        steep = slope[l, :, rows, :].reshape(cells * ROWS, hidden_units)
        pre = (act * steep).astype(jnp.bfloat16)
        result = against(pre, w_in[l]).reshape(cells, ROWS, chans)
        zonal[l][c][pl.ds(reaches[l], cells)] = result.astype(jnp.bfloat16)
        for side in sides:
            start_hop(l, c, 0, side)
        start_lat(l, c, result)

    def field(l, c):
        return zonal[l][c][pl.ds(reaches[l], cells)].astype(jnp.float32)

    def tapped(l, c):
        taps = [taps_ref[t, l, :].reshape(1, 1, chans) for t in range(5)]
        offset = dilation_ref[l]
        reach = reaches[l]
        place = lax.broadcasted_iota(jnp.int32, (cells, ROWS, chans), 1)
        here = field(l, c)
        if c + 1 < chunks:
            after = field(l, c + 1)
        else:
            after = halo_row(l, 0, lat == lat_count - 1)
        if c > 0:
            before = field(l, c - 1)
        else:
            before = halo_row(l, 1, lat == 0)
        from_north = pltpu.roll(jnp.where(place == 0, after, here), ROWS - 1, 1)
        from_south = pltpu.roll(jnp.where(place == ROWS - 1, before, here), 1, 1)
        window = zonal[l][c]
        ahead = window[pl.ds(reach + offset, cells)].astype(jnp.float32)
        behind = window[pl.ds(reach - offset, cells)].astype(jnp.float32)
        both = (taps[0] * ahead + taps[2] * behind).astype(jnp.bfloat16)
        return (
            both.astype(jnp.float32)
            + taps[1] * here
            + (taps[3] * from_north + taps[4] * from_south)
        )

    for c in order:
        conv_grad(layers - 1, c)

    for l in reversed(range(layers)):
        last = hop_count(l) - 1
        pieces = list(range(PIECES)) if l > 0 else []
        steps = [(hop, c) for hop in range(last) for c in order]
        ends = [(last, c) for c in order]

        def pass_on(step, side):
            arrive(l, step[1], step[0], side)
            start_hop(l, step[1], step[0] + 1, side)

        for piece in pieces:
            slope_piece(l - 1, piece)
        events = list(enumerate(steps + ends[:LEAD] + [None] * LAG))

        def relay(lag):
            for i, step in events:
                if step is not None:
                    if step[0] < last:
                        pass_on(step, sides[0])
                    turn_on(l, step[1], step[0])
                if 0 <= i - lag < len(steps):
                    pass_on(steps[i - lag], sides[1])

        pl.when(at_end == 1)(functools.partial(relay, LAG))
        pl.when(at_end == 0)(functools.partial(relay, 0))
        for i, c in enumerate(order):
            for side in sides:
                arrive(l, c, last, side)
            rows = pl.ds(c * ROWS, ROWS)
            total = grad[:, rows, :] + tapped(l, c)
            if l > 0:
                grad[:, rows, :] = total
                conv_grad(l - 1, c)
            else:
                out_ref[:, rows, :] = total.astype(jnp.bfloat16)
            if i + LEAD < chunks:
                turn_on(l, order[i + LEAD], last)

    for l in range(layers):
        for c in range(chunks):
            for hop in range(hop_count(l)):
                for side in range(2):
                    hop_copy(l, c, hop, side, 0).wait_send()

    @pl.when(turns_east + turns_west == 1)
    def _():
        for l in range(layers):
            for c in range(chunks):
                for hop in range(hop_count(l)):
                    turned_copy(l, c, hop).wait_send()

    for copy in lat_copies.values():
        copy.wait_send()


def whole_block(dims, reaches, *operands):
    layers, cells, lats, chans, hidden_units, _, _ = dims
    chunks = lats // ROWS
    dec_rows, values = operands[1].shape
    bf16, f32 = jnp.bfloat16, jnp.float32
    anywhere = pl.BlockSpec(memory_space=pl.ANY)
    return pl.pallas_call(
        functools.partial(kernel, dims, reaches),
        out_shape=jax.ShapeDtypeStruct((cells, lats, chans), bf16),
        in_specs=[
            pl.BlockSpec(memory_space=pltpu.SMEM),
            anywhere,
            anywhere,
            anywhere,
            anywhere,
            anywhere,
            pl.BlockSpec(memory_space=pltpu.VMEM),
        ],
        out_specs=pl.BlockSpec(memory_space=pltpu.VMEM),
        scratch_shapes=[
            pltpu.VMEM(
                (cells + 2 * reaches[l] + cells * len(hop_cells(reaches[l], cells)), ROWS, chans),
                bf16,
            )
            for l in range(layers)
            for c in range(chunks)
        ]
        + [
            pltpu.VMEM((layers, 2, cells, chans), bf16),
            pltpu.VMEM((layers, 2, cells, chans), bf16),
            pltpu.VMEM((dec_rows, values), bf16),
            pltpu.VMEM((chans, values), bf16),
            pltpu.VMEM((layers, cells * lats, chans), bf16),
            pltpu.VMEM((layers, chans, hidden_units), bf16),
            pltpu.VMEM((layers, hidden_units, chans), bf16),
            pltpu.VMEM((layers, cells, lats, hidden_units), f32),
            pltpu.VMEM((cells, lats, chans), f32),
            pltpu.SemaphoreType.DMA((3 * layers + 1,)),
            pltpu.SemaphoreType.DMA((2,)),
            pltpu.SemaphoreType.DMA((6 * layers * chunks,)),
            pltpu.SemaphoreType.DMA((9 * layers * chunks,)),
            pltpu.SemaphoreType.DMA((3 * layers * chunks,)),
            pltpu.SemaphoreType.DMA((2 * layers,)),
            pltpu.SemaphoreType.DMA((2 * layers,)),
        ],
        compiler_params=pltpu.CompilerParams(
            collective_id=0, has_side_effects=True, vmem_limit_bytes=60 << 20
        ),
    )(*operands)


def solution(mesh):
    lon_count, lat_count = mesh.shape["lon"], mesh.shape["lat"]

    def per_device(dec_cot, saved_conv, dec_weight, w_in, w_out, conv_taps, dilation):
        _, layers, cells, lats, chans = saved_conv.shape
        hidden_units = w_in.shape[2]
        dims = (layers, cells, lats, chans, hidden_units, lon_count, lat_count)
        reaches = (3 * cells,) * layers
        out = whole_block(
            dims,
            reaches,
            dilation,
            dec_cot[0].reshape(cells * lats, -1),
            saved_conv[0].reshape(layers, cells * lats, chans),
            dec_weight,
            w_in,
            w_out,
            conv_taps.transpose(1, 0, 2),
        )
        return out[None]

    in_specs = (
        P("segment", "lon", "lat", None),
        P("segment", None, "lon", "lat", None),
        P(),
        P(),
        P(),
        P(),
        P(),
    )
    out_specs = P("segment", "lon", "lat", None)
    return jax.shard_map(
        per_device, mesh=mesh, in_specs=in_specs, out_specs=out_specs, check_vma=False
    )
```

```python
import functools

import jax
import jax.numpy as jnp
from jax import lax
from jax.experimental import pallas as pl
from jax.experimental.pallas import tpu as pltpu
from jax.sharding import PartitionSpec as P

MESH = pl.DeviceIdType.MESH
ROWS = 8
RING = 12
LAG = 4
LEAD = 3
PIECES = 2


def gelu_slope(hidden):
    normal_cdf = 0.5 * (1.0 + lax.erf(hidden * 0.7071067811865476))
    density = jnp.exp(-0.5 * hidden * hidden) * 0.3989422804014327
    return normal_cdf + hidden * density


def against(left, right):
    return lax.dot_general(
        left, right, (((1,), (1,)), ((), ())), preferred_element_type=jnp.float32
    )


def hop_cells(reach, cells):
    counts = []
    while reach > 0:
        counts.append(min(reach, cells))
        reach -= cells
    return counts


def kernel(
    dims,
    reaches,
    dilation_ref,
    dec_cot_ref,
    saved_ref,
    dec_weight_ref,
    w_in_ref,
    w_out_ref,
    taps_ref,
    out_ref,
    *scratch,
):
    layers, cells, lats, chans, hidden_units, lon_count, lat_count = dims
    chunks = lats // ROWS
    zonal = [scratch[l * chunks : (l + 1) * chunks] for l in range(layers)]
    (
        edge,
        halo,
        dec_here,
        dec_weight,
        saved,
        w_in,
        w_out,
        slope,
        grad,
        load_sem,
        dec_sem,
        hop_send,
        hop_recv,
        via_send,
        lat_send,
        lat_recv,
    ) = scratch[layers * chunks :]

    seg = lax.axis_index("segment")
    lon = lax.axis_index("lon")
    lat = lax.axis_index("lat")
    east = lax.rem(lon + 1, lon_count)
    west = lax.rem(lon + lon_count - 1, lon_count)
    north = lax.rem(lat + 1, lat_count)
    south = lax.rem(lat + lat_count - 1, lat_count)

    def along(steps):
        return lax.rem(lon + lon_count + steps, lon_count)

    place_in_row = lax.rem(lon, RING)
    turns = seg
    turns_east = turns * (place_in_row // (RING - 1))
    turns_west = turns * ((RING - 1 - place_in_row) // (RING - 1))
    at_end = place_in_row // (RING - 1) + (RING - 1 - place_in_row) // (RING - 1)
    next_row, last_row = along(RING), along(-RING)

    barrier = pltpu.get_barrier_semaphore()
    for peer in (
        {"segment": 1 - seg},
        {"lon": east},
        {"lon": west},
        {"lat": north},
        {"lat": south},
        {"lon": next_row},
        {"lon": last_row},
        {"lon": along(RING - 1)},
        {"lon": along(1 - RING)},
    ):
        pl.semaphore_signal(barrier, inc=1, device_id=peer, device_id_type=MESH)

    loads = {}

    def load(name, src, dst):
        loads[name] = pltpu.make_async_copy(src, dst, load_sem.at[len(loads)])
        loads[name].start()

    for l in reversed(range(layers)):
        load(("saved", l), saved_ref.at[l], saved.at[l])
        load(("w_in", l), w_in_ref.at[l], w_in.at[l])
        if l == layers - 1:
            load("dec_weight", dec_weight_ref, dec_weight)
        load(("w_out", l), w_out_ref.at[l], w_out.at[l])

    def slope_piece(l, piece):
        if piece == 0:
            loads["saved", l].wait()
            loads["w_in", l].wait()
        span = cells // PIECES
        rows = span * lats
        hidden = jnp.dot(
            saved[l, pl.ds(piece * rows, rows), :],
            w_in[l],
            preferred_element_type=jnp.float32,
        )
        slope[l, pl.ds(piece * span, span)] = gelu_slope(hidden).reshape(
            span, lats, hidden_units
        )

    pl.semaphore_wait(barrier, 9)
    dec_copy = pltpu.make_async_remote_copy(
        src_ref=dec_cot_ref,
        dst_ref=dec_here,
        send_sem=dec_sem.at[0],
        recv_sem=dec_sem.at[1],
        device_id={"segment": 1 - seg},
        device_id_type=MESH,
    )
    dec_copy.start()
    for piece in range(PIECES):
        slope_piece(layers - 1, piece)
    loads["dec_weight"].wait()
    dec_copy.wait()
    handed = against(dec_here[...], dec_weight[...]).astype(jnp.bfloat16)
    grad[...] = handed.astype(jnp.float32).reshape(cells, lats, chans)

    order = [c for c in range(chunks) if 0 < c < chunks - 1] + [chunks - 1, 0]
    quick = place_in_row // (RING // 2)
    sides = (quick, 1 - quick)

    def hop_count(l):
        return len(hop_cells(reaches[l], cells))

    def slot_of(l, c, hop):
        return (l * chunks + c) * 3 + hop

    def either(choice, one, other):
        return other + choice * (one - other)

    def hop_copy(l, c, hop, side, turn):
        count, buf = hop_cells(reaches[l], cells)[hop], zonal[l][c]
        slot = slot_of(l, c, hop)
        own = reaches[l] + either(side, cells - count - hop * cells, hop * cells)
        landing = own + either(side, -cells, cells)
        via = cells + 2 * reaches[l] + hop * cells
        straight, round_corner = either(side, east, west), either(side, next_row, last_row)
        return pltpu.make_async_remote_copy(
            src_ref=buf.at[pl.ds(own, count)],
            dst_ref=buf.at[pl.ds(either(turn, via, landing), count)],
            send_sem=hop_send.at[2 * slot + side],
            recv_sem=hop_recv.at[
                either(turn, 6 * layers * chunks + slot, 2 * slot + side)
            ],
            device_id={"lon": either(turn, round_corner, straight)},
            device_id_type=MESH,
        )

    def turned_copy(l, c, hop):
        count, buf = hop_cells(reaches[l], cells)[hop], zonal[l][c]
        slot = slot_of(l, c, hop)
        via = cells + 2 * reaches[l] + hop * cells
        landing = reaches[l] + either(turns_east, -count - hop * cells, (hop + 1) * cells)
        return pltpu.make_async_remote_copy(
            src_ref=buf.at[pl.ds(via, count)],
            dst_ref=buf.at[pl.ds(landing, count)],
            send_sem=via_send.at[slot],
            recv_sem=hop_recv.at[2 * slot + turns_east],
            device_id={"lon": along(either(turns_east, 1 - RING, RING - 1))},
            device_id_type=MESH,
        )

    def start_hop(l, c, hop, side):
        hop_copy(l, c, hop, side, either(side, turns_east, turns_west)).start()

    def arrive(l, c, hop, side):
        hop_copy(l, c, hop, side, 0).wait_recv()

    def turn_on(l, c, hop):
        @pl.when(turns_east + turns_west == 1)
        def _():
            hop_copy(l, c, hop, turns_east, 1).wait_recv()
            turned_copy(l, c, hop).start()

    lat_copies = {}

    def start_lat(l, c, result):
        for which, chunk, row, peer in (
            (0, 0, 0, south),
            (1, chunks - 1, ROWS - 1, north),
        ):
            if c == chunk:
                edge[l, which] = result[:, row, :].astype(jnp.bfloat16)
                copy = pltpu.make_async_remote_copy(
                    src_ref=edge.at[l, which],
                    dst_ref=halo.at[l, which],
                    send_sem=lat_send.at[2 * l + which],
                    recv_sem=lat_recv.at[2 * l + which],
                    device_id={"lat": peer},
                    device_id_type=MESH,
                )
                copy.start()
                lat_copies[l, which] = copy

    def halo_row(l, which, outside):
        lat_copies[l, which].wait_recv()
        row = halo[l, which].astype(jnp.float32)
        row = jnp.where(outside, jnp.zeros_like(row), row)
        return row.reshape(cells, 1, chans)

    def conv_grad(l, c):
        if c == order[0]:
            loads["w_out", l].wait()
        rows = pl.ds(c * ROWS, ROWS)
        low = grad[:, rows, :].reshape(cells * ROWS, chans).astype(jnp.bfloat16)
        act = against(low, w_out[l])
        steep = slope[l, :, rows, :].reshape(cells * ROWS, hidden_units)
        pre = (act * steep).astype(jnp.bfloat16)
        result = against(pre, w_in[l]).reshape(cells, ROWS, chans)
        zonal[l][c][pl.ds(reaches[l], cells)] = result.astype(jnp.bfloat16)
        for side in sides:
            start_hop(l, c, 0, side)
        start_lat(l, c, result)

    def field(l, c):
        return zonal[l][c][pl.ds(reaches[l], cells)].astype(jnp.float32)

    def tapped(l, c):
        taps = [taps_ref[t, l, :].reshape(1, 1, chans) for t in range(5)]
        offset = dilation_ref[l]
        reach = reaches[l]
        place = lax.broadcasted_iota(jnp.int32, (cells, ROWS, chans), 1)
        here = field(l, c)
        if c + 1 < chunks:
            after = field(l, c + 1)
        else:
            after = halo_row(l, 0, lat == lat_count - 1)
        if c > 0:
            before = field(l, c - 1)
        else:
            before = halo_row(l, 1, lat == 0)
        from_north = pltpu.roll(jnp.where(place == 0, after, here), ROWS - 1, 1)
        from_south = pltpu.roll(jnp.where(place == ROWS - 1, before, here), 1, 1)
        window = zonal[l][c]
        ahead = window[pl.ds(reach + offset, cells)].astype(jnp.float32)
        behind = window[pl.ds(reach - offset, cells)].astype(jnp.float32)
        both = (taps[0] * ahead + taps[2] * behind).astype(jnp.bfloat16)
        return (
            both.astype(jnp.float32)
            + taps[1] * here
            + (taps[3] * from_north + taps[4] * from_south)
        )

    for c in order:
        conv_grad(layers - 1, c)

    for l in reversed(range(layers)):
        last = hop_count(l) - 1
        pieces = list(range(PIECES)) if l > 0 else []
        steps = [(hop, c) for hop in range(last) for c in order]
        ends = [(last, c) for c in order]

        def pass_on(step, side):
            arrive(l, step[1], step[0], side)
            start_hop(l, step[1], step[0] + 1, side)

        for piece in pieces:
            slope_piece(l - 1, piece)
        events = list(enumerate(steps + ends[:LEAD] + [None] * LAG))

        def relay(lag):
            for i, step in events:
                if step is not None:
                    if step[0] < last:
                        pass_on(step, sides[0])
                    turn_on(l, step[1], step[0])
                if 0 <= i - lag < len(steps):
                    pass_on(steps[i - lag], sides[1])

        pl.when(at_end == 1)(functools.partial(relay, LAG))
        pl.when(at_end == 0)(functools.partial(relay, 0))
        for i, c in enumerate(order):
            for side in sides:
                arrive(l, c, last, side)
            rows = pl.ds(c * ROWS, ROWS)
            total = grad[:, rows, :] + tapped(l, c)
            if l > 0:
                grad[:, rows, :] = total
                conv_grad(l - 1, c)
            else:
                out_ref[:, rows, :] = total.astype(jnp.bfloat16)
            if i + LEAD < chunks:
                turn_on(l, order[i + LEAD], last)

    for l in range(layers):
        for c in range(chunks):
            for hop in range(hop_count(l)):
                for side in range(2):
                    hop_copy(l, c, hop, side, 0).wait_send()

    @pl.when(turns_east + turns_west == 1)
    def _():
        for l in range(layers):
            for c in range(chunks):
                for hop in range(hop_count(l)):
                    turned_copy(l, c, hop).wait_send()

    for copy in lat_copies.values():
        copy.wait_send()


def whole_block(dims, reaches, *operands):
    layers, cells, lats, chans, hidden_units, _, _ = dims
    chunks = lats // ROWS
    dec_rows, values = operands[1].shape
    bf16, f32 = jnp.bfloat16, jnp.float32
    anywhere = pl.BlockSpec(memory_space=pl.ANY)
    return pl.pallas_call(
        functools.partial(kernel, dims, reaches),
        out_shape=jax.ShapeDtypeStruct((cells, lats, chans), bf16),
        in_specs=[
            pl.BlockSpec(memory_space=pltpu.SMEM),
            anywhere,
            anywhere,
            anywhere,
            anywhere,
            anywhere,
            pl.BlockSpec(memory_space=pltpu.VMEM),
        ],
        out_specs=pl.BlockSpec(memory_space=pltpu.VMEM),
        scratch_shapes=[
            pltpu.VMEM(
                (cells + 2 * reaches[l] + cells * len(hop_cells(reaches[l], cells)), ROWS, chans),
                bf16,
            )
            for l in range(layers)
            for c in range(chunks)
        ]
        + [
            pltpu.VMEM((layers, 2, cells, chans), bf16),
            pltpu.VMEM((layers, 2, cells, chans), bf16),
            pltpu.VMEM((dec_rows, values), bf16),
            pltpu.VMEM((chans, values), bf16),
            pltpu.VMEM((layers, cells * lats, chans), bf16),
            pltpu.VMEM((layers, chans, hidden_units), bf16),
            pltpu.VMEM((layers, hidden_units, chans), bf16),
            pltpu.VMEM((layers, cells, lats, hidden_units), f32),
            pltpu.VMEM((cells, lats, chans), f32),
            pltpu.SemaphoreType.DMA((3 * layers + 1,)),
            pltpu.SemaphoreType.DMA((2,)),
            pltpu.SemaphoreType.DMA((6 * layers * chunks,)),
            pltpu.SemaphoreType.DMA((9 * layers * chunks,)),
            pltpu.SemaphoreType.DMA((3 * layers * chunks,)),
            pltpu.SemaphoreType.DMA((2 * layers,)),
            pltpu.SemaphoreType.DMA((2 * layers,)),
        ],
        compiler_params=pltpu.CompilerParams(
            collective_id=0, has_side_effects=True, vmem_limit_bytes=60 << 20
        ),
    )(*operands)


def solution(mesh):
    lon_count, lat_count = mesh.shape["lon"], mesh.shape["lat"]

    def per_device(dec_cot, saved_conv, dec_weight, w_in, w_out, conv_taps, dilation):
        _, layers, cells, lats, chans = saved_conv.shape
        hidden_units = w_in.shape[2]
        dims = (layers, cells, lats, chans, hidden_units, lon_count, lat_count)
        reaches = (3 * cells,) * layers
        out = whole_block(
            dims,
            reaches,
            dilation,
            dec_cot[0].reshape(cells * lats, -1),
            saved_conv[0].reshape(layers, cells * lats, chans),
            dec_weight,
            w_in,
            w_out,
            conv_taps.transpose(1, 0, 2),
        )
        return out[None]

    in_specs = (
        P("segment", "lon", "lat", None),
        P("segment", None, "lon", "lat", None),
        P(),
        P(),
        P(),
        P(),
        P(),
    )
    out_specs = P("segment", "lon", "lat", None)
    return jax.shard_map(
        per_device, mesh=mesh, in_specs=in_specs, out_specs=out_specs, check_vma=False
    )
```
